32 devices in a mesh: rep: 16 (over z, x, core), shard: 2 (over y).
Axes of the slice: x: 2, y: 2, z: 4, core: 2. Of those that a mesh axis runs over, the one named last changes fastest.
Arguments:
- tokens: bfloat16 [8192, 576], P(('rep', 'shard')), may hold values from -6 to 6
- doc_ids: int32 [16, 512], P('rep', 'shard'), may hold values from 0 to 3, never falling along the last dimension, each value on 1 to 256 neighbouring positions
- gain_attn: float32 [576], P('shard'), may hold values from 0.5 to 1.5
- w_query: bfloat16 [576, 576], P('shard'), may hold values from -0.25 to 0.25
- w_key: bfloat16 [576, 192], P('shard'), may hold values from -0.25 to 0.25
- w_value: bfloat16 [576, 192], P('shard'), may hold values from -0.25 to 0.25
- w_out: bfloat16 [576, 576], P('shard'), may hold values from -1 to 1
- gain_ffn: float32 [576], P('shard'), may hold values from 0.5 to 1.5
- w_gate: bfloat16 [576, 1536], P('shard'), may hold values from -0.25 to 0.25
- w_up: bfloat16 [576, 1536], P('shard'), may hold values from -0.25 to 0.25
- w_down: bfloat16 [1536, 576], P('shard'), may hold values from -0.3125 to 0.3125
- cotangent: bfloat16 [8192, 576], P(('rep', 'shard')), may hold values from -6 to 6
Outputs:
- output: bfloat16 [8192, 576], P(('rep', 'shard'))
- grad_tokens: float32 [8192, 576], P(('rep', 'shard'))
- grad_gain_attn: float32 [576], P('shard')
- grad_w_query: float32 [576, 576], P('shard')
- grad_w_key: float32 [576, 192], P('shard')
- grad_w_value: float32 [576, 192], P('shard')
- grad_w_out: float32 [576, 576], P('shard')
- grad_gain_ffn: float32 [576], P('shard')
- grad_w_gate: float32 [576, 1536], P('shard')
- grad_w_up: float32 [576, 1536], P('shard')
- grad_w_down: float32 [1536, 576], P('shard')
The draws below stay inside these ranges and needn't reach their ends.
Inputs may be any that keep to these rules, and one draw needn't show every extreme that they name: `doc_ids`: along each sequence the document number never falls; every document has at most 256 tokens, and some document has exactly that many.
All inputs are finite; a program needn't handle non-finite values.
Results may differ from the reference program's by a relative error of at most 0.04.
Values may be sent and summed in bfloat16 or wider, within the bound.
No kernel may reach another device: no remote copies, remote signals or barrier semaphores. Data moves between devices by JAX's collectives and lax.ppermute only.
A program may use at most 128 MiB of HBM per device.

```python
import math
import jax
import jax.numpy as jnp
import numpy as np
from jax import lax

D = 576
HEADS = 9
KV_HEADS = 3
HD = 64
FF = 1536
DOCS = 4
GROUP = 3
LENGTH = 512
TOKENS = 8192
N_REP = 16


def block_scale(key, extent, pieces, least, top_value):
    def one(dim, blocks):
        steps = jax.random.uniform(jax.random.fold_in(jax.random.fold_in(key, 6), dim), (blocks,), jnp.float32, least / len(pieces), top_value / len(pieces))
        return jnp.repeat(jnp.exp(steps), extent[dim] // blocks).reshape((-1,) + (1,) * (len(extent) - dim - 1))

    factor_of = one(*pieces[0])
    for cut in pieces[1:]:
        factor_of = factor_of * one(*cut)
    return factor_of


def profile(number_of, total, limit, slope):
    weights = [(1 << 20) // math.isqrt(rank ** slope) + 1 for rank in range(2, number_of + 1)]
    surplus, given = total - limit - (number_of - 1), [1] * (number_of - 1)
    while surplus > 0:
        candidates = [i for i in range(number_of - 1) if given[i] < limit]
        pool, remaining = sum([weights[i] for i in candidates]), surplus
        for i in candidates:
            extra = min(limit - given[i], max(1, remaining * weights[i] // pool), surplus)
            given[i] = given[i] + extra
            surplus = surplus - extra
    return np.array([limit] + given)


def uneven_parts(own_key, amount, total, limit, skew):
    if amount == 2:
        one = jax.random.randint(own_key, (), max(1, total - limit), min(limit, total - 1) + 1)
        return jnp.stack([one, total - one])
    tallies = jnp.asarray(profile(amount, total, limit, skew), jnp.int32)
    twos = (amount - 1) // 2
    giver, taker = tallies[1:1 + 2 * twos:2], tallies[2:2 + 2 * twos:2]
    slack = jnp.minimum(giver - 1, limit - taker)
    passed = jax.random.randint(jax.random.fold_in(own_key, 1), (twos,), 0, 1 << 20) % (slack + 1)
    tallies = tallies.at[1:1 + 2 * twos:2].set(giver - passed).at[2:2 + 2 * twos:2].set(taker + passed)
    return tallies[jax.random.permutation(jax.random.fold_in(own_key, 2), amount)]


def noise(rng, extent, width, most, cuts=(), kind=jnp.bfloat16):
    loudness = block_scale(rng, extent, cuts, -0.22, 0.18) if cuts else 1.0
    values = jax.random.normal(rng, extent, jnp.float32) * width * loudness
    return jnp.minimum(jnp.maximum(values, -most), most).astype(kind)


def setup_inputs(seed: int = 0) -> dict:
    arg_keys = jax.random.split(jax.random.key(seed), 13)
    return {
        "tokens": noise(arg_keys[0], (TOKENS, D), 1.0, 6.0, ((0, 32),)),
        "doc_ids": jax.vmap(lambda own: jnp.searchsorted(jnp.cumsum(uneven_parts(own, DOCS, LENGTH, LENGTH // 2, 0)), jnp.arange(LENGTH), side="right"))(jax.random.split(arg_keys[1], N_REP)).reshape((N_REP, LENGTH)).astype(jnp.int32),
        "gain_attn": jnp.clip(1.0 + 0.1 * jax.random.normal(arg_keys[2], (D,), jnp.float32), 0.5, 1.5),
        "w_query": noise(arg_keys[3], (D, HEADS * HD), D ** -0.5, 0.25, ((0, 2),)),
        "w_key": noise(arg_keys[4], (D, KV_HEADS * HD), D ** -0.5, 0.25, ((0, 2),)),
        "w_value": noise(arg_keys[5], (D, KV_HEADS * HD), D ** -0.5, 0.25, ((0, 2),)),
        "w_out": noise(arg_keys[6], (HEADS * HD, D), (D // 16) ** -0.5, 1.0, ((0, 2),)),
        "gain_ffn": jnp.clip(1.0 + 0.1 * jax.random.normal(arg_keys[7], (D,), jnp.float32), 0.5, 1.5),
        "w_gate": noise(arg_keys[8], (D, FF), D ** -0.5, 0.25, ((0, 2),)),
        "w_up": noise(arg_keys[9], (D, FF), D ** -0.5, 0.25, ((0, 2),)),
        "w_down": noise(arg_keys[10], (FF, D), (FF // 4) ** -0.5, 0.3125, ((0, 2),)),
        "cotangent": noise(arg_keys[11], (TOKENS, D), 1.0, 6.0, ((0, 32),)),
    }


EPSILON = 1e-05
ROPE_BASE = 100000.0

def rope_tables(positions):
    halves = jnp.arange(HD // 2, dtype=jnp.float32)
    inverse = jnp.power(jnp.float32(ROPE_BASE), -2.0 * halves / HD)
    angles = positions[:, None] * inverse[None, :]
    return (jnp.cos(angles), jnp.sin(angles))

def rotate(values, cosine, sine, direction):
    row_count = values.shape[0]
    shaped = values.reshape(row_count, -1, HD)
    front_half = shaped[:, :, :HD // 2]
    back_half = shaped[:, :, HD // 2:]
    cosine_rows = cosine[:, None, :]
    sine_rows = direction * sine[:, None, :]
    result = jnp.concatenate([front_half * cosine_rows - back_half * sine_rows, back_half * cosine_rows + front_half * sine_rows], axis=2)
    return result.reshape(row_count, -1)

def norm_forward(values, gain):
    scale_inv = lax.rsqrt(lax.optimization_barrier(jnp.mean(values * values, axis=1, keepdims=True)) + EPSILON)
    normed = values * scale_inv
    return (normed, scale_inv, (normed * gain[None, :]).astype(jnp.bfloat16))

def norm_backward(grad_out, normed, scale_inv, gain):
    grad_normed = grad_out * gain[None, :]
    grad_in = scale_inv * (grad_normed - normed * lax.optimization_barrier(jnp.mean(grad_normed * normed, axis=1, keepdims=True)))
    return (grad_in, lax.optimization_barrier(jnp.sum(grad_out * normed, axis=0)))

def masked_scores(query_group, key_head, allowed):
    scores = jnp.einsum('gqd,kd->gqk', query_group.astype(jnp.float32), key_head.astype(jnp.float32)) * (1.0 / math.sqrt(HD))
    return jnp.where(allowed[None], scores, -1e+30)

def group_forward(query_group, key_head, value_head, allowed):
    scores = masked_scores(query_group, key_head, allowed)
    peak = lax.optimization_barrier(jnp.max(scores, axis=2, keepdims=True))
    total = lax.optimization_barrier(jnp.sum(jnp.exp(scores - peak), axis=2, keepdims=True))
    log_total = peak + jnp.log(total)
    probs = jnp.exp(scores - log_total).astype(jnp.bfloat16)
    attended = jnp.einsum('gqk,kd->gqd', probs.astype(jnp.float32), value_head.astype(jnp.float32))
    return (attended, log_total[..., 0])

def group_backward(query_group, key_head, value_head, log_total, grad_group, delta_group, allowed):
    scores = masked_scores(query_group, key_head, allowed)
    probs = jnp.exp(scores - log_total[..., None])
    probs_low = probs.astype(jnp.bfloat16)
    grad_float = grad_group.astype(jnp.float32)
    grad_value = jnp.einsum('gqk,gqd->kd', probs_low.astype(jnp.float32), grad_float)
    grad_probs = jnp.einsum('gqd,kd->gqk', grad_float, value_head.astype(jnp.float32))
    grad_scores = (probs * (grad_probs - delta_group[..., None]) * (1.0 / math.sqrt(HD))).astype(jnp.bfloat16)
    scores_float = grad_scores.astype(jnp.float32)
    grad_query = jnp.einsum('gqk,kd->gqd', scores_float, key_head.astype(jnp.float32))
    grad_key = jnp.einsum('gqk,gqd->kd', scores_float, query_group.astype(jnp.float32))
    return (grad_query, grad_key, grad_value)

def sequence_pass(seq_tokens, seq_grad, seq_docs, weights):
    w_query, w_key, w_value, w_out, w_gate, w_up, w_down, gain_attn, gain_ffn = weights
    count = seq_tokens.shape[0]
    token_index = jnp.arange(count, dtype=jnp.int32)
    cosine, sine = rope_tables(token_index.astype(jnp.float32))
    allowed = (seq_docs[:, None] == seq_docs[None, :]) & (token_index[None, :] <= token_index[:, None])
    hidden_in = seq_tokens.astype(jnp.float32)
    normed_one, inv_one, hidden_one = norm_forward(hidden_in, gain_attn)
    queries = rotate(jnp.dot(hidden_one, w_query, preferred_element_type=jnp.float32), cosine, sine, 1.0).astype(jnp.bfloat16)
    keys_all = rotate(jnp.dot(hidden_one, w_key, preferred_element_type=jnp.float32), cosine, sine, 1.0).astype(jnp.bfloat16)
    values_all = jnp.dot(hidden_one, w_value, preferred_element_type=jnp.float32).astype(jnp.bfloat16)
    query_groups = queries.reshape(count, KV_HEADS, GROUP, HD).transpose(1, 2, 0, 3)
    key_heads = keys_all.reshape(count, KV_HEADS, HD).transpose(1, 0, 2)
    value_heads = values_all.reshape(count, KV_HEADS, HD).transpose(1, 0, 2)
    attended, log_totals = lax.map(lambda operands: group_forward(operands[0], operands[1], operands[2], allowed), (query_groups, key_heads, value_heads))
    attn_low = attended.transpose(2, 0, 1, 3).reshape(count, HEADS * HD).astype(jnp.bfloat16)
    resid = hidden_in + jnp.dot(attn_low, w_out, preferred_element_type=jnp.float32)
    normed_two, inv_two, hidden_two = norm_forward(resid, gain_ffn)
    gate = jnp.dot(hidden_two, w_gate, preferred_element_type=jnp.float32)
    upward = jnp.dot(hidden_two, w_up, preferred_element_type=jnp.float32)
    sigmoid = jax.nn.sigmoid(gate)
    active = gate * sigmoid
    inner = (active * upward).astype(jnp.bfloat16)
    output = (resid + jnp.dot(inner, w_down, preferred_element_type=jnp.float32)).astype(jnp.bfloat16)
    grad_seed = seq_grad.astype(jnp.float32)
    grad_down = jnp.dot(inner.T, seq_grad, preferred_element_type=jnp.float32)
    grad_inner = jnp.dot(seq_grad, w_down.T, preferred_element_type=jnp.float32)
    grad_gate = (grad_inner * upward * (sigmoid * (1.0 + gate * (1.0 - sigmoid)))).astype(jnp.bfloat16)
    grad_upward = (grad_inner * active).astype(jnp.bfloat16)
    grad_w_gate = jnp.dot(hidden_two.T, grad_gate, preferred_element_type=jnp.float32)
    grad_w_up = jnp.dot(hidden_two.T, grad_upward, preferred_element_type=jnp.float32)
    grad_hidden_two = jnp.dot(grad_gate, w_gate.T, preferred_element_type=jnp.float32) + jnp.dot(grad_upward, w_up.T, preferred_element_type=jnp.float32)
    grad_norm_two, grad_gain_two = norm_backward(grad_hidden_two, normed_two, inv_two, gain_ffn)
    grad_resid = grad_seed + grad_norm_two
    grad_resid_low = grad_resid.astype(jnp.bfloat16)
    grad_w_out = jnp.dot(attn_low.T, grad_resid_low, preferred_element_type=jnp.float32)
    grad_attn = jnp.dot(grad_resid_low, w_out.T, preferred_element_type=jnp.float32).astype(jnp.bfloat16)
    delta = (grad_attn.astype(jnp.float32) * attn_low.astype(jnp.float32)).reshape(count, KV_HEADS, GROUP, HD).sum(axis=3).transpose(1, 2, 0)
    grad_groups = grad_attn.reshape(count, KV_HEADS, GROUP, HD).transpose(1, 2, 0, 3)
    grad_q, grad_k, grad_v = lax.map(lambda operands: group_backward(operands[0], operands[1], operands[2], operands[3], operands[4], operands[5], allowed), (query_groups, key_heads, value_heads, log_totals, grad_groups, delta))
    grad_q = grad_q.transpose(2, 0, 1, 3).reshape(count, HEADS * HD)
    grad_k = grad_k.transpose(1, 0, 2).reshape(count, KV_HEADS * HD)
    grad_v = grad_v.transpose(1, 0, 2).reshape(count, KV_HEADS * HD)
    grad_query = rotate(grad_q, cosine, sine, -1.0).astype(jnp.bfloat16)
    grad_key = rotate(grad_k, cosine, sine, -1.0).astype(jnp.bfloat16)
    grad_value = grad_v.astype(jnp.bfloat16)
    grad_w_query = jnp.dot(hidden_one.T, grad_query, preferred_element_type=jnp.float32)
    grad_w_key = jnp.dot(hidden_one.T, grad_key, preferred_element_type=jnp.float32)
    grad_w_value = jnp.dot(hidden_one.T, grad_value, preferred_element_type=jnp.float32)
    grad_hidden_one = jnp.dot(grad_query, w_query.T, preferred_element_type=jnp.float32) + jnp.dot(grad_key, w_key.T, preferred_element_type=jnp.float32) + jnp.dot(grad_value, w_value.T, preferred_element_type=jnp.float32)
    grad_norm_one, grad_gain_one = norm_backward(grad_hidden_one, normed_one, inv_one, gain_attn)
    grad_input = grad_resid + grad_norm_one
    grads = (grad_w_query, grad_w_key, grad_w_value, grad_w_out, grad_w_gate, grad_w_up, grad_down, grad_gain_one, grad_gain_two)
    return (output, grad_input, grads)

def reference(tokens, doc_ids, gain_attn, w_query, w_key, w_value, w_out, gain_ffn, w_gate, w_up, w_down, cotangent):
    weights = (w_query, w_key, w_value, w_out, w_gate, w_up, w_down, gain_attn, gain_ffn)
    token_seqs = tokens.reshape(N_REP, LENGTH, D)
    grad_seqs = cotangent.reshape(N_REP, LENGTH, D)
    zeros = tuple((jnp.zeros(weight.shape, jnp.float32) for weight in weights))

    def per_sequence(carry, operands):
        output, grad_input, grads = sequence_pass(operands[0], operands[1], operands[2], weights)
        return (tuple((total + part for total, part in zip(carry, grads))), (output, grad_input))
    final, (outputs, grad_inputs) = lax.scan(per_sequence, zeros, (token_seqs, grad_seqs, doc_ids))
    return (outputs.reshape(TOKENS, D), grad_inputs.reshape(TOKENS, D), final[7], final[0], final[1], final[2], final[3], final[8], final[4], final[5], final[6])
```

```python
import math

import jax
import jax.numpy as jnp
from jax import lax
from jax.sharding import PartitionSpec as P

HD = 64
EPSILON = 1e-05
ROPE_BASE = 100000.0
F32 = jnp.float32
BF16 = jnp.bfloat16


def mm(a, b):
    return jnp.dot(a, b, preferred_element_type=F32)


def mm_t(a, b):
    return lax.dot_general(a, b, (((0,), (0,)), ((), ())), preferred_element_type=F32)


def mm_nt(a, b):
    return lax.dot_general(a, b, (((1,), (1,)), ((), ())), preferred_element_type=F32)


def swap(value, axis, mask, size):
    return lax.ppermute(value, axis, [(i, i ^ mask) for i in range(size)])


def after(value, *others):
    return lax.optimization_barrier((value,) + others)[0]


def rope_tables(positions):
    halves = jnp.arange(HD // 2, dtype=F32)
    inverse = jnp.power(F32(ROPE_BASE), -2.0 * halves / HD)
    angles = positions[:, None] * inverse[None, :]
    return (jnp.cos(angles), jnp.sin(angles))


def rotate(values, cosine, sine, direction):
    row_count = values.shape[0]
    shaped = values.reshape(row_count, -1, HD)
    front = shaped[:, :, : HD // 2]
    back = shaped[:, :, HD // 2 :]
    cos = cosine[:, None, :]
    sin = direction * sine[:, None, :]
    result = jnp.concatenate([front * cos - back * sin, back * cos + front * sin], axis=2)
    return result.reshape(row_count, -1)


def norm_forward(values, gain):
    scale = lax.rsqrt(jnp.mean(values * values, axis=1, keepdims=True) + EPSILON)
    normed = values * scale
    return (normed, scale, (normed * gain[None, :]).astype(BF16))


def norm_backward(grad_out, normed, scale, gain):
    grad_normed = grad_out * gain[None, :]
    grad_in = scale * (
        grad_normed - normed * jnp.mean(grad_normed * normed, axis=1, keepdims=True)
    )
    return (grad_in, jnp.sum(grad_out * normed, axis=0))


class Comm:
    def __init__(self, n_rep, n_shard):
        self.rep, self.shard = n_rep, n_shard
        self.rep_index = lax.axis_index("rep")
        self.shard_index = lax.axis_index("shard")
        self.core = self.rep_index % 2
        self.rest = self.rep_index // 2
        self.n_rest = n_rep // 2

    def pieces(self, own, send_of, axis, size, shift=0):
        got = [own]
        for mask in range(1, size):
            got.append(swap(send_of(mask), axis, mask << shift, self.axis_size(axis)))
        return got

    def axis_size(self, axis):
        return self.rep if axis == "rep" else self.shard

    def ordered(self, got, index):
        stacked = jnp.stack(got)
        picks = [
            lax.dynamic_index_in_dim(stacked, lax.bitwise_xor(index, k), 0, keepdims=False)
            for k in range(len(got))
        ]
        return picks

    def gather_shard(self, value):
        got = self.pieces(value, lambda m: value, "shard", self.shard)
        return self.ordered(got, self.shard_index)

    def gather_weight(self, value, axis, quarters):
        parts = jnp.split(value, quarters, axis)
        mine = lax.dynamic_index_in_dim(
            jnp.stack(parts), self.rep_index % quarters, 0, keepdims=False
        )
        others = [
            swap(mine, "shard", m, self.shard) for m in range(1, self.shard)
        ]
        cur = jnp.stack(others)
        mask = quarters // 2
        held = [cur]
        while mask >= 1:
            held = held + [swap(h, "rep", mask, self.rep) for h in held]
            mask //= 2
        order = []
        for j in range(quarters):
            flip = 0
            for b in range(int(math.log2(quarters))):
                if j >> b & 1:
                    flip |= (quarters // 2) >> b
            order.append(flip)
        by_flip = [None] * quarters
        for j, flip in enumerate(order):
            by_flip[flip] = held[j]
        stacked = jnp.stack(by_flip)
        full = [
            lax.dynamic_index_in_dim(
                stacked, lax.bitwise_xor(self.rep_index % quarters, k), 0, keepdims=False
            )
            for k in range(quarters)
        ]
        wide = jnp.concatenate(full, axis=axis + 1)
        everyone = [value] + [wide[m] for m in range(self.shard - 1)]
        return jnp.concatenate(self.ordered(everyone, self.shard_index), axis=0)

    def reduce_grad(self, value, core_axis, rest_axis):
        halves = jnp.stack(jnp.split(value.astype(BF16), 2, core_axis + 1))
        take = lambda v, i: lax.dynamic_index_in_dim(v, i, 0, keepdims=False)
        got = swap(take(halves, 1 - self.core), "rep", 1, self.rep)
        cur = (take(halves, self.core).astype(F32) + got.astype(F32)).astype(BF16)
        total = take(cur, self.shard_index).astype(F32)
        for m in range(1, self.shard):
            sent = take(cur, lax.bitwise_xor(self.shard_index, m))
            total = total + swap(sent, "shard", m, self.shard).astype(F32)
        size = total.shape[rest_axis]
        pads = [(0, 0), (0, 0)]
        pads[rest_axis] = (0, -size % self.n_rest)
        chunks = jnp.stack(jnp.split(jnp.pad(total.astype(BF16), pads), self.n_rest, rest_axis))
        mine = take(chunks, self.rest).astype(F32)
        for m in range(1, self.n_rest):
            sent = take(chunks, lax.bitwise_xor(self.rest, m))
            mine = mine + swap(sent, "rep", m << 1, self.rep).astype(F32)
        mine = mine.astype(BF16)
        got = [mine] + [swap(mine, "rep", m << 1, self.rep) for m in range(1, self.n_rest)]
        half = jnp.concatenate(self.ordered(got, self.rest), axis=rest_axis)
        half = lax.slice_in_dim(half, 0, size, axis=rest_axis)
        other = swap(half, "rep", 1, self.rep)
        both = [
            jnp.where(self.core == 0, half, other),
            jnp.where(self.core == 0, other, half),
        ]
        return jnp.concatenate(both, axis=core_axis).astype(F32)

    def sum_small(self, value):
        mask = 1
        while mask < self.shard:
            value = value + swap(value, "shard", mask, self.shard)
            mask *= 2
        mask = 1
        while mask < self.rep:
            value = value + swap(value, "rep", mask, self.rep)
            mask *= 2
        return value


def masked_scores(query_group, key_head, allowed):
    scores = jnp.einsum(
        "gqd,kd->gqk", query_group, key_head, preferred_element_type=F32
    ) * (1.0 / math.sqrt(HD))
    return jnp.where(allowed[None], scores, -1e30)


def group_forward(query_group, key_head, value_head, allowed):
    scores = masked_scores(query_group, key_head, allowed)
    peak = jnp.max(scores, axis=2, keepdims=True)
    total = jnp.sum(jnp.exp(scores - peak), axis=2, keepdims=True)
    log_total = peak + jnp.log(total)
    probs = jnp.exp(scores - log_total).astype(BF16)
    attended = jnp.einsum("gqk,kd->gqd", probs, value_head, preferred_element_type=F32)
    return (attended, log_total[..., 0])


def group_backward(query_group, key_head, value_head, log_total, grad_group, delta_group, allowed):
    scores = masked_scores(query_group, key_head, allowed)
    probs = jnp.exp(scores - log_total[..., None])
    probs_low = probs.astype(BF16)
    grad_value = jnp.einsum("gqk,gqd->kd", probs_low, grad_group, preferred_element_type=F32)
    grad_probs = jnp.einsum("gqd,kd->gqk", grad_group, value_head, preferred_element_type=F32)
    grad_scores = (probs * (grad_probs - delta_group[..., None]) * (1.0 / math.sqrt(HD))).astype(
        BF16
    )
    grad_query = jnp.einsum("gqk,kd->gqd", grad_scores, key_head, preferred_element_type=F32)
    grad_key = jnp.einsum("gqk,gqd->kd", grad_scores, query_group, preferred_element_type=F32)
    return (grad_query, grad_key, grad_value)


def per_device(n_rep, n_shard, *args):
    (
        tokens,
        doc_ids,
        gain_attn,
        w_query,
        w_key,
        w_value,
        w_out,
        gain_ffn,
        w_gate,
        w_up,
        w_down,
        cotangent,
    ) = args
    comm = Comm(n_rep, n_shard)
    rows = tokens.shape[0]
    width = tokens.shape[1]
    q_cols, kv_cols, ff = w_query.shape[1], w_key.shape[1], w_gate.shape[1]
    kv_heads = kv_cols // HD
    group = q_cols // kv_cols
    keys = rows * n_shard

    gains = jnp.stack(comm.gather_shard(jnp.stack([gain_attn, gain_ffn])), axis=1).reshape(2, -1)
    gain_one, gain_two = gains[0], gains[1]
    docs_all = jnp.stack(comm.gather_shard(doc_ids.reshape(rows))).reshape(-1)
    own_docs = doc_ids.reshape(rows)

    w_in = comm.gather_weight(jnp.concatenate([w_query, w_key, w_value], axis=1), 1, 2)
    tokens_first = after(tokens, w_in)
    tokens_all = jnp.concatenate(comm.gather_shard(tokens_first), axis=0)
    w_out_full = comm.gather_weight(after(w_out, w_in), 0, 2)
    w_gu = comm.gather_weight(after(jnp.concatenate([w_gate, w_up], axis=1), w_in), 1, 4)
    w_dn = comm.gather_weight(after(w_down, w_gu), 0, 4)

    first_row = comm.shard_index * rows
    query_index = first_row + jnp.arange(rows, dtype=jnp.int32)
    key_index = jnp.arange(keys, dtype=jnp.int32)
    cosine, sine = rope_tables(query_index.astype(F32))
    cosine_all, sine_all = rope_tables(key_index.astype(F32))

    hidden_in = tokens.astype(F32)
    normed_one, inv_one, hidden_one = norm_forward(hidden_in, gain_one)
    hidden_all = norm_forward(tokens_all.astype(F32), gain_one)[2]
    queries = rotate(mm(hidden_one, w_in[:, :q_cols]), cosine, sine, 1.0).astype(BF16)
    kv_all = mm(hidden_all, w_in[:, q_cols:])
    keys_all = rotate(kv_all[:, :kv_cols], cosine_all, sine_all, 1.0).astype(BF16)
    values_all = kv_all[:, kv_cols:].astype(BF16)
    allowed = (own_docs[:, None] == docs_all[None, :]) & (
        key_index[None, :] <= query_index[:, None]
    )
    query_groups = queries.reshape(rows, kv_heads, group, HD).transpose(1, 2, 0, 3)
    key_heads = keys_all.reshape(keys, kv_heads, HD).transpose(1, 0, 2)
    value_heads = values_all.reshape(keys, kv_heads, HD).transpose(1, 0, 2)
    attended, log_totals = lax.map(
        lambda o: group_forward(o[0], o[1], o[2], allowed),
        (query_groups, key_heads, value_heads),
    )
    attn_low = attended.transpose(2, 0, 1, 3).reshape(rows, q_cols).astype(BF16)
    resid = hidden_in + mm(attn_low, w_out_full)
    normed_two, inv_two, hidden_two = norm_forward(resid, gain_two)
    gate_up = mm(hidden_two, w_gu)
    gate, upward = gate_up[:, :ff], gate_up[:, ff:]
    sigmoid = jax.nn.sigmoid(gate)
    active = gate * sigmoid
    inner = (active * upward).astype(BF16)
    output = (resid + mm(inner, w_dn)).astype(BF16)

    grad_down = comm.reduce_grad(mm_t(inner, cotangent).reshape(n_shard, -1, width), 0, 0)
    grad_seed = cotangent.astype(F32)
    grad_inner = mm_nt(cotangent, w_dn)
    grad_gu = jnp.concatenate(
        [
            (grad_inner * upward * (sigmoid * (1.0 + gate * (1.0 - sigmoid)))).astype(BF16),
            (grad_inner * active).astype(BF16),
        ],
        axis=1,
    )
    grad_w_gu = comm.reduce_grad(mm_t(hidden_two, grad_gu).reshape(n_shard, -1, 2 * ff), 0, 1)
    grad_hidden_two = mm_nt(grad_gu, w_gu)
    grad_norm_two, grad_gain_two = norm_backward(grad_hidden_two, normed_two, inv_two, gain_two)
    grad_resid = grad_seed + grad_norm_two
    grad_resid_low = grad_resid.astype(BF16)
    grad_w_out = comm.reduce_grad(mm_t(attn_low, grad_resid_low).reshape(n_shard, -1, width), 0, 0)
    grad_attn = mm_nt(grad_resid_low, w_out_full).astype(BF16)
    delta = (
        (grad_attn.astype(F32) * attn_low.astype(F32))
        .reshape(rows, kv_heads, group, HD)
        .sum(axis=3)
        .transpose(1, 2, 0)
    )
    grad_groups = grad_attn.reshape(rows, kv_heads, group, HD).transpose(1, 2, 0, 3)
    grad_q, grad_k, grad_v = lax.map(
        lambda o: group_backward(o[0], o[1], o[2], o[3], o[4], o[5], allowed),
        (query_groups, key_heads, value_heads, log_totals, grad_groups, delta),
    )
    grad_q = grad_q.transpose(2, 0, 1, 3).reshape(rows, q_cols)
    grad_kv = jnp.concatenate(
        [
            grad_k.transpose(1, 0, 2).reshape(n_shard, rows, kv_cols),
            grad_v.transpose(1, 0, 2).reshape(n_shard, rows, kv_cols),
        ],
        axis=2,
    )
    take = lambda i: lax.dynamic_index_in_dim(grad_kv, i, 0, keepdims=False)
    kv_sum = take(comm.shard_index)
    for m in range(1, n_shard):
        sent = take(lax.bitwise_xor(comm.shard_index, m)).astype(BF16)
        kv_sum = kv_sum + swap(sent, "shard", m, n_shard).astype(F32)
    grad_in_cat = jnp.concatenate(
        [
            rotate(grad_q, cosine, sine, -1.0).astype(BF16),
            rotate(kv_sum[:, :kv_cols], cosine, sine, -1.0).astype(BF16),
            kv_sum[:, kv_cols:].astype(BF16),
        ],
        axis=1,
    )
    in_cols = q_cols + 2 * kv_cols
    grad_w_in = mm_t(hidden_one, grad_in_cat).reshape(n_shard, -1, in_cols)
    pad = -in_cols % (128 * comm.n_rest)
    grad_w_in = comm.reduce_grad(jnp.pad(grad_w_in, ((0, 0), (0, 0), (0, pad))), 0, 1)
    grad_hidden_one = mm_nt(grad_in_cat, w_in)
    grad_norm_one, grad_gain_one = norm_backward(grad_hidden_one, normed_one, inv_one, gain_one)
    grad_input = grad_resid + grad_norm_one
    gain_sums = comm.sum_small(jnp.stack([grad_gain_one, grad_gain_two]))
    own = gain_attn.shape[0]
    gain_own = lax.dynamic_slice(gain_sums, (0, comm.shard_index * own), (2, own))
    return (
        output,
        grad_input,
        gain_own[0],
        grad_w_in[:, :q_cols],
        grad_w_in[:, q_cols : q_cols + kv_cols],
        grad_w_in[:, q_cols + kv_cols : in_cols],
        grad_w_out,
        gain_own[1],
        grad_w_gu[:, :ff],
        grad_w_gu[:, ff:],
        grad_down,
    )


def solution(mesh):
    tok, vec, mat = P(("rep", "shard"), None), P("shard"), P("shard", None)
    in_specs = (tok, P("rep", "shard"), vec, mat, mat, mat, mat, vec, mat, mat, mat, tok)
    out_specs = (tok, tok, vec, mat, mat, mat, mat, vec, mat, mat, mat)
    n_rep, n_shard = mesh.shape["rep"], mesh.shape["shard"]

    def body(*args):
        return per_device(n_rep, n_shard, *args)

    return jax.shard_map(body, mesh=mesh, in_specs=in_specs, out_specs=out_specs, check_vma=False)
```
